512 devices in a mesh: mem: 16 (over y, core), lat: 8 (over x, z_hi), lon: 4 (over z_lo).
Axes of the slice: x: 4, y: 8, z: 8 (z_hi: 2, z_lo: 4; z = z_hi * 4 + z_lo), core: 2. Of those that a mesh axis runs over, the one named last changes fastest.
Arguments:
- members: bfloat16 [32, 8, 256, 512], P('mem', None, 'lat', 'lon'), may hold values from -6 to 6
- increment: float32 [8, 256, 512], P(None, 'lat', 'lon'), may hold values from -6 to 6
Outputs:
- covariance_product: float32 [8, 256, 512], P(None, 'lat', 'lon')
The draws below stay inside these ranges and needn't reach their ends.
All inputs are finite; a program needn't handle non-finite values.
Results may differ from the reference program's by a relative error of at most 0.0003.
Values sent between devices are 32-bit elements; how exact they have to be, the bound alone decides.
No kernel may reach another device: no remote copies, remote signals or barrier semaphores. Data moves between devices by JAX's collectives and lax.ppermute only.
A program may use at most 64 MiB of HBM per device.

```python
import jax
import jax.numpy as jnp
from jax import lax

MEMBERS = 32
LEV = 8
ITERS = 4
NLAT = 256
NLON = 512


def shard_levels(stream_key, extent, split, low, top_value):
    gain, own = 1.0, jax.random.fold_in(stream_key, 6)
    for dim, blocks in split:
        steps = jnp.exp(jax.random.uniform(jax.random.fold_in(own, dim), (blocks,), jnp.float32, low / len(split), top_value / len(split)))
        gain = gain * jnp.repeat(steps, extent[dim] // blocks).reshape([-1 if axis == dim else 1 for axis in range(len(extent))])
    return gain


def centred(own_key, dims, deviation, limit, cuts=(), held_as=jnp.bfloat16):
    drawn = jax.random.normal(own_key, dims, jnp.float32) * deviation
    if len(cuts) > 0:
        drawn = shard_levels(own_key, dims, cuts, -0.22, 0.18) * drawn
    return jnp.clip(drawn, min=-limit, max=limit).astype(held_as)


def setup_inputs(seed: int = 0) -> dict:
    seeds = jax.random.split(jax.random.key(seed), 3)
    members = centred(seeds[0], (MEMBERS, LEV, NLAT, NLON), 1.0, 6.0, ((0, 16), (2, 8), (3, 4)))
    increment = centred(seeds[1], (LEV, NLAT, NLON), 1.0, 6.0, ((1, 8), (2, 4)), jnp.float32)
    return dict(members=members, increment=increment)


factors = (1, 2, 4)
stiffnesses = (1.0, 2.0, 4.0)
weights = (0.5, 0.3, 0.2)


def coarsen(values_now, factor):
    if factor == 1:
        return values_now
    dims_now = values_now.shape
    blocks = values_now.reshape(dims_now[:-2] + (dims_now[-2] // factor, factor, dims_now[-1] // factor, factor))
    return jnp.mean(blocks, axis=(-3, -1))


def refine(values_now, factor):
    if factor == 1:
        return values_now
    return jnp.repeat(jnp.repeat(values_now, factor, axis=-2), factor, axis=-1)


def diffuse(source, stiffness):
    smoothed = source
    for sweeps in range(ITERS):
        padded = jnp.pad(smoothed, [(0, 0)] * (source.ndim - 2) + [(1, 1), (0, 0)])
        beside_all = padded[..., :-2, :] + padded[..., 2:, :]
        beside_all = beside_all + jnp.roll(smoothed, 1, axis=-1) + jnp.roll(smoothed, -1, axis=-1)
        smoothed = (source + stiffness * beside_all) / (1.0 + 4.0 * stiffness)
    return smoothed


def reference(members, increment):
    def accumulate(running, member):
        member_field = member.astype(jnp.float32)
        for factor, stiffness, weight in zip(factors, stiffnesses, weights):
            coarse = diffuse(coarsen(member_field * increment, factor), stiffness)
            running = running + weight * member_field * refine(coarse, factor)
        return running, None

    initial = jnp.zeros(increment.shape, jnp.float32)
    running, unused = lax.scan(accumulate, initial, members)
    return running / (MEMBERS - 1)
```

```python
import functools

import jax
import jax.numpy as jnp
from jax import lax
from jax.experimental import pallas as pl
from jax.experimental.pallas import tpu as pltpu
from jax.sharding import PartitionSpec as P

ITERS = 4
factors = (1, 2, 4)
stiffnesses = (1.0, 2.0, 4.0)
weights = (0.5, 0.3, 0.2)
scales = tuple(w / (1.0 + 4.0 * k) for w, k in zip(weights, stiffnesses))

LEV = 8
ROWS = 32
LANES = 128
PLANES = 16
MAIN = 8
CORNERS = 2


def lane_ids():
    return lax.broadcasted_iota(jnp.int32, (PLANES, LANES), 1)


def in_range(lane, start, width):
    return ((lane - start) & (LANES - 1)) < width


def pack_kernel(members_ref, increment_ref, held_ref, s1_ref, s2_ref, s4_ref, lon_ref, lat_ref, wide_ref):
    lane = lane_ids()
    here, count = lax.axis_index("lon"), lax.axis_size("lon")
    odd = lax.rem(lax.axis_index("lat"), 2)
    wide_ref[...] = members_ref[...].astype(jnp.float32)
    for row in range(ROWS):
        inc = increment_ref[pl.ds(row, LEV, stride=ROWS), :] * scales[0]
        for m in range(2):
            value = wide_ref[pl.ds(m * LEV * ROWS + row, LEV, stride=ROWS), :]
            held_ref[row, m * LEV : (m + 1) * LEV, :] = value
            s1_ref[row, m * LEV : (m + 1) * LEV, :] = value * inc
    for row in range(ROWS // 2):
        pair = s1_ref[2 * row] + s1_ref[2 * row + 1]
        pair = pair + jnp.where((lane & 1) == 0, pltpu.roll(pair, LANES - 1, 1), pltpu.roll(pair, 1, 1))
        s2_ref[row] = pair * (0.25 * scales[1] / scales[0])
    for row in range(ROWS // 4):
        pair = s2_ref[2 * row] + s2_ref[2 * row + 1]
        pair = pair + jnp.where((lane & 2) == 0, pltpu.roll(pair, LANES - 2, 1), pltpu.roll(pair, 2, 1))
        s4_ref[row] = pair * (0.25 * scales[2] / scales[1])

    tiles = []
    for ref, factor in ((s1_ref, 1), (s2_ref, 2), (s4_ref, 4)):
        width = ITERS * factor
        first = last = jnp.zeros((PLANES, LANES), jnp.float32)
        for row in range(ROWS // factor):
            turned = pltpu.roll(ref[row], width * row, 1) if row else ref[row]
            first = jnp.where(in_range(lane, width * row, width), turned, first)
            last = jnp.where(in_range(lane, width * row - width, width), turned, last)
        tiles.append((first, last))
    even = (lane & 1) == 0
    blank = jnp.zeros((2, PLANES, LANES), jnp.float32)
    lon_ref[here] = blank
    lon_ref[lax.rem(here + 2, count)] = blank
    for side, to in ((0, lax.rem(here + count - 1, count)), (1, lax.rem(here + 1, count))):
        lon_ref[to, 0] = tiles[0][side]
        lon_ref[to, 1] = jnp.where(even, tiles[1][side], tiles[2][side])

    for slot, tail in ((odd, True), (1 - odd, False)):
        for k in range(ITERS):
            at = lambda ref: ref[ref.shape[0] - ITERS + k] if tail else ref[k]
            lat_ref[slot, k] = at(s1_ref)
            lat_ref[slot, ITERS + k] = jnp.where(even, at(s2_ref), at(s4_ref))


def side_tiles(got_ref, lane):
    here, count = lax.axis_index("lon"), lax.axis_size("lon")
    even = (lane & 1) == 0
    out = []
    for of in (lax.rem(here + 1, count), lax.rem(here + count - 1, count)):
        mixed = got_ref[of, 1]
        out.append(
            (
                got_ref[of, 0],
                jnp.where(even, mixed, pltpu.roll(mixed, 1, 1)),
                jnp.where(even, pltpu.roll(mixed, LANES - 1, 1), mixed),
            )
        )
    return out


def beside(right, left, lane, width, row):
    both = jnp.where(in_range(lane, width * row, LANES // 2), right, left)
    return pltpu.roll(both, (LANES - width * row) % LANES, 1)


CORNER_PLACES = ((2, 0, 0, 16), (2, 1, 64, 16), (1, 0, 24, 8), (1, 1, 88, 8), (0, 0, 36, 4), (0, 1, 100, 4))


def corner_kernel(got_ref, lat_ref, out0_ref, out1_ref):
    lane = lane_ids()
    odd = lax.rem(lax.axis_index("lat"), 2)
    right, left = side_tiles(got_ref, lane)
    out0_ref[:MAIN] = lat_ref[0]
    out1_ref[:MAIN] = lat_ref[1]
    made = []
    for tail in (True, False):
        tiles = []
        for t in range(CORNERS):
            tile = jnp.zeros((PLANES, LANES), jnp.float32)
            for band, which, shift, width in CORNER_PLACES:
                row = 2 * t + which + (ROWS // factors[band] - ITERS if tail else 0)
                halo = beside(right[band], left[band], lane, width, row)
                halo = pltpu.roll(halo, shift, 1) if shift else halo
                tile = jnp.where(in_range(lane, shift - width, 2 * width), halo, tile)
            tiles.append(tile)
        made.append(tiles)
    is_odd = (lane * 0 + odd) == 1
    for t in range(CORNERS):
        tail, head = made[0][t], made[1][t]
        out0_ref[MAIN + t] = jnp.where(is_odd, head, tail)
        out1_ref[MAIN + t] = jnp.where(is_odd, tail, head)


def diffuse_kernel(held_ref, s1_ref, s2_ref, s4_ref, got_ref, lat0_ref, lat1_ref, out_ref, edge_ref, *scratch):
    lane = lane_ids()
    place, places = lax.axis_index("lat"), lax.axis_size("lat")
    odd = lax.rem(place, 2)
    right, left = side_tiles(got_ref, lane)
    edge_ref[0] = lat0_ref[...]
    edge_ref[1] = lat1_ref[...]
    even = (lane & 1) == 0
    above, below = edge_ref.at[1 - odd], edge_ref.at[odd]
    keep_above = jnp.where(place > 0, 1.0, 0.0).astype(jnp.float32)
    keep_below = jnp.where(place < places - 1, 1.0, 0.0).astype(jnp.float32)

    for band, (factor, stiffness) in enumerate(zip(factors, stiffnesses)):
        source, field = scratch[2 * band], scratch[2 * band + 1]
        own, rows, width = (s1_ref, s2_ref, s4_ref)[band], ROWS // factor, ITERS * factor
        for row in range(rows):
            source[ITERS + row, 0] = own[row]
            source[ITERS + row, 1] = beside(right[band], left[band], lane, width, row)
        for base, edge in ((0, above), (ITERS + rows, below)):
            for k in range(ITERS):
                if band == 0:
                    value = edge[k]
                else:
                    value = edge[ITERS + k]
                    turned = pltpu.roll(value, 1 if band == 1 else LANES - 1, 1)
                    value = jnp.where(even, value, turned) if band == 1 else jnp.where(even, turned, value)
                source[base + k, 0] = value
                shift = next(s for b, w, s, _ in CORNER_PLACES if b == band and w == k % 2)
                corner = edge[MAIN + k // 2]
                source[base + k, 1] = pltpu.roll(corner, LANES - shift, 1) if shift else corner
        low, high = lane < factor, lane >= LANES - factor
        for sweep in range(1, ITERS + 1):
            old = source if sweep == 1 else field
            gain = stiffness if sweep == 1 else stiffness / (1.0 + 4.0 * stiffness)
            start, stop = sweep, rows + 2 * ITERS - sweep
            halves = (0,) if sweep == ITERS else (0, 1)
            before = [old[start - 1, h] for h in halves]
            now = [old[start, 0], old[start, 1]]
            for row in range(start, stop):
                after = [old[row + 1, 0], old[row + 1, 1]]
                up = [pltpu.roll(v, factor, 1) for v in now]
                down = [pltpu.roll(v, LANES - factor, 1) for v in now]
                for h in halves:
                    total = before[h] + after[h]
                    total = total + jnp.where(low, up[1 - h], up[h])
                    total = total + jnp.where(high, down[1 - h], down[h])
                    value = source[row, h] + gain * total
                    if row < ITERS:
                        value = value * keep_above
                    elif row >= ITERS + rows:
                        value = value * keep_below
                    field[row, h] = value
                before, now = now, after
    for row in range(ROWS):
        total = scratch[1][ITERS + row, 0] + scratch[3][ITERS + row // 2, 0] + scratch[5][ITERS + row // 4, 0]
        total = total * held_ref[row]
        out_ref[pl.ds(row, LEV, stride=ROWS), :] = total[:LEV] + total[LEV:]


def tiles_of(*dims):
    return jax.ShapeDtypeStruct(dims + (PLANES, LANES), jnp.float32)


def vmem(count):
    return [pl.BlockSpec(memory_space=pltpu.VMEM)] * count


def body(members, increment):
    columns = lax.axis_size("lon")
    parts = lax.axis_size("mem")
    rows_of = lax.axis_size("lat")
    held, s1, s2, s4, to_lon, to_lat = pl.pallas_call(
        pack_kernel,
        out_shape=(
            tiles_of(ROWS),
            tiles_of(ROWS),
            tiles_of(ROWS // 2),
            tiles_of(ROWS // 4),
            tiles_of(columns, 2),
            tiles_of(2, MAIN),
        ),
        in_specs=vmem(2),
        out_specs=tuple(vmem(6)),
        scratch_shapes=[pltpu.VMEM((2 * LEV * ROWS, LANES), jnp.float32)],
        name="pack",
    )(members.reshape(2 * LEV * ROWS, LANES), increment.reshape(LEV * ROWS, LANES))
    from_lon = lax.all_to_all(to_lon, "lon", 0, 0)
    out0, out1 = pl.pallas_call(
        corner_kernel,
        out_shape=(tiles_of(MAIN + CORNERS), tiles_of(MAIN + CORNERS)),
        in_specs=vmem(2),
        out_specs=tuple(vmem(2)),
        name="corner",
    )(from_lon, to_lat)
    swap0 = [(i, i ^ 1) for i in range(rows_of)]
    swap1 = [(i, ((i + 1) ^ 1) - 1) for i in range(1, rows_of - 1)]
    in0 = lax.ppermute(out0, "lat", swap0)
    in1 = lax.ppermute(out1, "lat", swap1)
    fields = []
    for factor in factors:
        fields += [pltpu.VMEM((ROWS // factor + 2 * ITERS, 2, PLANES, LANES), jnp.float32)] * 2
    partial_value = pl.pallas_call(
        diffuse_kernel,
        out_shape=jax.ShapeDtypeStruct((LEV * ROWS, LANES), jnp.float32),
        in_specs=vmem(7),
        out_specs=vmem(1)[0],
        scratch_shapes=[pltpu.VMEM((2, MAIN + CORNERS, PLANES, LANES), jnp.float32)] + fields,
        name="diffuse",
    )(held, s1, s2, s4, from_lon, in0, in1)
    member_count = members.shape[0] * parts
    chunk = (parts, LEV * ROWS // parts, LANES)
    mine = jnp.sum(lax.all_to_all(partial_value.reshape(chunk), "mem", 0, 0), axis=0)
    mine = mine * (1.0 / (member_count - 1))
    whole = lax.all_to_all(jnp.broadcast_to(mine[None], chunk), "mem", 0, 0)
    return whole.reshape(LEV, ROWS, LANES)


def solution(mesh):
    return jax.shard_map(
        body,
        mesh=mesh,
        in_specs=(P("mem", None, "lat", "lon"), P(None, "lat", "lon")),
        out_specs=P(None, "lat", "lon"),
        check_vma=False,
    )
```

```python
import functools

import jax
import jax.numpy as jnp
from jax import lax
from jax.experimental import pallas as pl
from jax.experimental.pallas import tpu as pltpu
from jax.sharding import PartitionSpec as P

ITERS = 4
factors = (1, 2, 4)
stiffnesses = (1.0, 2.0, 4.0)
weights = (0.5, 0.3, 0.2)
scales = tuple(w / (1.0 + 4.0 * k) for w, k in zip(weights, stiffnesses))

LEV = 8
ROWS = 32
LANES = 128
PLANES = 16
GRANT = 16 * 1024 * 1024
EDGE = 9
CORNER = EDGE - 1


def lane_ids():
    return lax.broadcasted_iota(jnp.int32, (PLANES, LANES), 1)


def in_range(lane, start, width):
    return ((lane - start) & (LANES - 1)) < width


def pack_kernel(
    members_hbm, increment_hbm, held_ref, s1_ref, s2_ref, s4_ref, lon_ref, lat_ref, members_ref, increment_ref, wide_ref, sems
):
    lane = lane_ids()
    here, count = lax.axis_index("lon"), lax.axis_size("lon")
    odd = lax.rem(lax.axis_index("lat"), 2)
    half = LEV * ROWS
    fetches = [pltpu.make_async_copy(increment_hbm, increment_ref, sems.at[0])]
    for m in range(2):
        part = pl.ds(m * half, half)
        fetches.append(pltpu.make_async_copy(members_hbm.at[part], members_ref.at[part], sems.at[1 + m]))
    for fetch in fetches:
        fetch.start()
    fetches[0].wait()
    for m in range(2):
        fetches[1 + m].wait()
        wide_ref[m * half : (m + 1) * half] = members_ref[m * half : (m + 1) * half].astype(jnp.float32)
        for row in range(ROWS):
            inc = increment_ref[pl.ds(row, LEV, stride=ROWS), :] * scales[0]
            value = wide_ref[pl.ds(m * half + row, LEV, stride=ROWS), :]
            held_ref[row, m * LEV : (m + 1) * LEV, :] = value
            s1_ref[row, m * LEV : (m + 1) * LEV, :] = value * inc
    for row in range(ROWS // 2):
        pair = s1_ref[2 * row] + s1_ref[2 * row + 1]
        pair = pair + jnp.where((lane & 1) == 0, pltpu.roll(pair, LANES - 1, 1), pltpu.roll(pair, 1, 1))
        s2_ref[row] = pair * (0.25 * scales[1] / scales[0])
    for row in range(ROWS // 4):
        pair = s2_ref[2 * row] + s2_ref[2 * row + 1]
        pair = pair + jnp.where((lane & 2) == 0, pltpu.roll(pair, LANES - 2, 1), pltpu.roll(pair, 2, 1))
        s4_ref[row] = pair * (0.25 * scales[2] / scales[1])

    tiles = []
    for ref, factor in ((s1_ref, 1), (s2_ref, 2), (s4_ref, 4)):
        width = ITERS * factor
        first = last = jnp.zeros((PLANES, LANES), jnp.float32)
        for row in range(ROWS // factor):
            turned = pltpu.roll(ref[row], width * row, 1) if row else ref[row]
            first = jnp.where(in_range(lane, width * row, width), turned, first)
            last = jnp.where(in_range(lane, width * row - width, width), turned, last)
        tiles.append((first, last))
    even = (lane & 1) == 0
    blank = jnp.zeros((2, PLANES, LANES), jnp.float32)
    lon_ref[here] = blank
    lon_ref[lax.rem(here + 2, count)] = blank
    for side, to in ((0, lax.rem(here + count - 1, count)), (1, lax.rem(here + 1, count))):
        lon_ref[to, 0] = tiles[0][side]
        lon_ref[to, 1] = jnp.where(even, tiles[1][side], tiles[2][side])

    for slot, tail in ((odd, True), (1 - odd, False)):
        for k in range(ITERS):
            at = lambda ref: ref[ref.shape[0] - ITERS + k] if tail else ref[k]
            lat_ref[slot, k] = at(s1_ref)
            lat_ref[slot, ITERS + k] = jnp.where(even, at(s2_ref), at(s4_ref))


def side_tiles(got_ref, lane):
    here, count = lax.axis_index("lon"), lax.axis_size("lon")
    even = (lane & 1) == 0
    out = []
    for of in (lax.rem(here + 1, count), lax.rem(here + count - 1, count)):
        mixed = got_ref[of, 1]
        out.append(
            (
                got_ref[of, 0],
                jnp.where(even, mixed, pltpu.roll(mixed, 1, 1)),
                jnp.where(even, pltpu.roll(mixed, LANES - 1, 1), mixed),
            )
        )
    return out


def beside(right, left, lane, width, row):
    both = jnp.where(in_range(lane, width * row, LANES // 2), right, left)
    return pltpu.roll(both, (LANES - width * row) % LANES, 1)


CORNER_PLACES = ((2, 1, 0), (2, 2, 20), (2, 3, 32), (1, 1, 42), (1, 2, 52), (1, 3, 58), (0, 1, 63), (0, 2, 68), (0, 3, 71))
SHIFTS = {(band, distance): shift for band, distance, shift in CORNER_PLACES}


def corner_kernel(got_ref, lat_ref, out0_ref, out1_ref):
    lane = lane_ids()
    odd = lax.rem(lax.axis_index("lat"), 2)
    right, left = side_tiles(got_ref, lane)
    out0_ref[:CORNER] = lat_ref[0]
    out1_ref[:CORNER] = lat_ref[1]
    made = []
    for tail in (True, False):
        tile = jnp.zeros((PLANES, LANES), jnp.float32)
        for band, distance, shift in CORNER_PLACES:
            factor = factors[band]
            width = factor * (ITERS - distance)
            row = ROWS // factor - distance if tail else distance - 1
            halo = beside(right[band], left[band], lane, ITERS * factor, row)
            halo = pltpu.roll(halo, shift, 1) if shift else halo
            tile = jnp.where(in_range(lane, shift - width, 2 * width), halo, tile)
        made.append(tile)
    is_odd = (lane * 0 + odd) == 1
    out0_ref[CORNER] = jnp.where(is_odd, made[1], made[0])
    out1_ref[CORNER] = jnp.where(is_odd, made[0], made[1])


def sweep_row(before, now, after, base, factor, gain, lane, halves=(0, 1)):
    low, high = lane < factor, lane >= LANES - factor
    up = [pltpu.roll(v, factor, 1) for v in now]
    down = [pltpu.roll(v, LANES - factor, 1) for v in now]
    out = []
    for h in halves:
        total = before[h] + after[h]
        total = total + jnp.where(low, up[1 - h], up[h])
        total = total + jnp.where(high, down[1 - h], down[h])
        out.append(base[h] + gain * total)
    return out


def gain_of(stiffness, sweep):
    return stiffness if sweep == 1 else stiffness / (1.0 + 4.0 * stiffness)


def inner_kernel(s1_ref, s2_ref, s4_ref, got_ref, *levels):
    lane = lane_ids()
    right, left = side_tiles(got_ref, lane)
    for band, (factor, stiffness) in enumerate(zip(factors, stiffnesses)):
        level, own, rows = levels[band], (s1_ref, s2_ref, s4_ref)[band], ROWS // factor
        for row in range(rows):
            level[0, row, 0] = own[row]
            level[0, row, 1] = beside(right[band], left[band], lane, ITERS * factor, row)
        for sweep in range(1, ITERS + 1):
            halves = (0,) if sweep == ITERS else (0, 1)
            load = lambda row: [level[sweep - 1, row, h] for h in (0, 1)]
            if rows - sweep <= sweep:
                continue
            before, now = load(sweep - 1), load(sweep)
            for row in range(sweep, rows - sweep):
                after = load(row + 1)
                base = [level[0, row, h] for h in halves]
                value = sweep_row(before, now, after, base, factor, gain_of(stiffness, sweep), lane, halves)
                for h in halves:
                    level[sweep, row, h] = value[h]
                before, now = now, after


def outer_kernel(held_ref, lat0_ref, lat1_ref, level1_ref, level2_ref, level4_ref, out_ref, edge_ref, ends_ref):
    lane = lane_ids()
    even = (lane & 1) == 0
    place, places = lax.axis_index("lat"), lax.axis_size("lat")
    odd = lax.rem(place, 2)
    edge_ref[0] = lat0_ref[...]
    edge_ref[1] = lat1_ref[...]
    found = []
    for band, (factor, stiffness) in enumerate(zip(factors, stiffnesses)):
        level, rows = (level1_ref, level2_ref, level4_ref)[band], ROWS // factor
        ends = {}
        for top in (True, False):
            edge = edge_ref.at[1 - odd] if top else edge_ref.at[odd]
            keep = jnp.where(place > 0 if top else place < places - 1, 1.0, 0.0).astype(jnp.float32)
            row_at = (lambda d: -d) if top else (lambda d: rows - 1 + d)
            outside = {}
            for distance in range(1, ITERS + 1):
                k = ITERS - distance if top else distance - 1
                if band == 0:
                    value = edge[k]
                else:
                    value = edge[ITERS + k]
                    turned = pltpu.roll(value, 1 if band == 1 else LANES - 1, 1)
                    value = jnp.where(even, value, turned) if band == 1 else jnp.where(even, turned, value)
                corner = edge[CORNER]
                shift = SHIFTS.get((band, distance), 0)
                outside[row_at(distance)] = [value, pltpu.roll(corner, LANES - shift, 1) if shift else corner]
            latest = dict(outside)
            for sweep in range(1, ITERS + 1):
                halves = (0,) if sweep == ITERS else (0, 1)

                def load(row):
                    return latest[row] if row in latest else [level[sweep - 1, row, h] for h in (0, 1)]

                new = {}
                for distance in range(1 - sweep, ITERS + 1 - sweep):
                    row = row_at(distance)
                    base = outside[row] if distance > 0 else [level[0, row, h] for h in halves]
                    value = sweep_row(
                        load(row - 1), load(row), load(row + 1), base, factor, gain_of(stiffness, sweep), lane, halves
                    )
                    new[row] = [v * keep for v in value] if distance > 0 else value
                latest = new
            for row in range(ITERS):
                at = row if top else ITERS + row
                ends_ref[band, at] = latest[row if top else rows - ITERS + row][0]
    def final(band, row):
        rows = ROWS // factors[band]
        if row < ITERS:
            return ends_ref[band, row]
        if row >= rows - ITERS:
            return ends_ref[band, row - rows + 2 * ITERS]
        return (level1_ref, level2_ref, level4_ref)[band][ITERS, row, 0]

    for row in range(ROWS):
        total = (final(0, row) + final(1, row // 2) + final(2, row // 4)) * held_ref[row]
        out_ref[pl.ds(row, LEV, stride=ROWS), :] = total[:LEV] + total[LEV:]


def tiles_of(*dims):
    return pltpu.VMEM(dims + (PLANES, LANES), jnp.float32)


def on_chip(kernel, name, out_shape, scratch_shapes=(), held_in=pltpu.VMEM, bundles=1000):
    several = isinstance(out_shape, tuple)
    spec = pl.BlockSpec(memory_space=pltpu.VMEM)

    def call(*operands):
        return pl.pallas_call(
            kernel,
            out_shape=out_shape,
            in_specs=[spec if held_in == pltpu.VMEM else pl.BlockSpec(memory_space=pl.ANY)] * len(operands),
            out_specs=(spec,) * len(out_shape) if several else spec,
            scratch_shapes=scratch_shapes,
            compiler_params=pltpu.CompilerParams(vmem_limit_bytes=GRANT),
            cost_estimate=pl.CostEstimate(flops=bundles * 4096, bytes_accessed=bundles * 1024, transcendentals=0),
            name=name,
        )(*[pltpu.with_memory_space_constraint(x, held_in) for x in operands])

    return call


def body(members, increment):
    columns = lax.axis_size("lon")
    parts = lax.axis_size("mem")
    rows_of = lax.axis_size("lat")
    held, s1, s2, s4, to_lon, to_lat = on_chip(
        pack_kernel,
        "pack",
        (
            tiles_of(ROWS),
            tiles_of(ROWS),
            tiles_of(ROWS // 2),
            tiles_of(ROWS // 4),
            tiles_of(columns, 2),
            tiles_of(2, CORNER),
        ),
        [
            pltpu.VMEM((2 * LEV * ROWS, LANES), jnp.bfloat16),
            pltpu.VMEM((LEV * ROWS, LANES), jnp.float32),
            pltpu.VMEM((2 * LEV * ROWS, LANES), jnp.float32),
            pltpu.SemaphoreType.DMA((3,)),
        ],
        held_in=pltpu.HBM,
    )(members.reshape(2 * LEV * ROWS, LANES), increment.reshape(LEV * ROWS, LANES))
    from_lon = lax.all_to_all(to_lon, "lon", 0, 0)
    out0, out1 = on_chip(corner_kernel, "corner", (tiles_of(EDGE), tiles_of(EDGE)))(from_lon, to_lat)
    swap0 = [(i, i ^ 1) for i in range(rows_of)]
    swap1 = [(i, ((i + 1) ^ 1) - 1) for i in range(1, rows_of - 1)]
    in0 = lax.ppermute(out0, "lat", swap0)
    in1 = lax.ppermute(out1, "lat", swap1)
    levels = on_chip(
        inner_kernel, "inner", tuple(tiles_of(ITERS + 1, ROWS // factor, 2) for factor in factors), bundles=3000
    )(s1, s2, s4, from_lon)
    partial_value = on_chip(
        outer_kernel,
        "outer",
        pltpu.VMEM((LEV * ROWS, LANES), jnp.float32),
        [tiles_of(2, EDGE), tiles_of(3, 2 * ITERS)],
    )(held, in0, in1, *levels)
    member_count = members.shape[0] * parts
    chunk = (parts, LEV * ROWS // parts, LANES)
    mine = jnp.sum(lax.all_to_all(partial_value.reshape(chunk), "mem", 0, 0), axis=0)
    mine = mine * (1.0 / (member_count - 1))
    whole = lax.all_to_all(jnp.broadcast_to(mine[None], chunk), "mem", 0, 0)
    return whole.reshape(LEV, ROWS, LANES)


def solution(mesh):
    return jax.shard_map(
        body,
        mesh=mesh,
        in_specs=(P("mem", None, "lat", "lon"), P(None, "lat", "lon")),
        out_specs=P(None, "lat", "lon"),
        check_vma=False,
    )
```

```python
import math

import jax
import jax.numpy as jnp
from jax import lax
from jax.experimental import pallas as pl
from jax.experimental.pallas import tpu as pltpu
from jax.sharding import PartitionSpec as P

ITERS = 4
factors = (1, 2, 4)
stiffnesses = (1.0, 2.0, 4.0)
weights = (0.5, 0.3, 0.2)
scales = tuple(w / (1.0 + 4.0 * k) for w, k in zip(weights, stiffnesses))

POLY = []
for stiffness in stiffnesses:
    step = stiffness / (1.0 + 4.0 * stiffness)
    series = [step**j for j in range(ITERS)] + [step ** (ITERS - 1) * stiffness]
    POLY.append([[math.comb(i + k, i) * series[i + k] for k in range(ITERS + 1 - i)] for i in range(ITERS + 1)])

LEV = 8
ROWS = 32
LANES = 128
PLANES = 16
GRANT = 16 * 1024 * 1024
EDGE = 9
CORNER = EDGE - 1


def lane_ids():
    return lax.broadcasted_iota(jnp.int32, (PLANES, LANES), 1)


def in_range(lane, start, width):
    return ((lane - start) & (LANES - 1)) < width


def pack_kernel(
    members_hbm, increment_hbm, held_ref, s1_ref, s2_ref, s4_ref, lon_ref, members_ref, increment_ref, wide_ref, sems
):
    lane = lane_ids()
    here, count = lax.axis_index("lon"), lax.axis_size("lon")
    half = LEV * ROWS
    fetches = [pltpu.make_async_copy(increment_hbm, increment_ref, sems.at[0])]
    for m in range(2):
        part = pl.ds(m * half, half)
        fetches.append(pltpu.make_async_copy(members_hbm.at[part], members_ref.at[part], sems.at[1 + m]))
    for fetch in fetches:
        fetch.start()
    fetches[0].wait()
    for m in range(2):
        fetches[1 + m].wait()
        wide_ref[m * half : (m + 1) * half] = members_ref[m * half : (m + 1) * half].astype(jnp.float32)
        for row in range(ROWS):
            inc = increment_ref[pl.ds(row, LEV, stride=ROWS), :] * scales[0]
            value = wide_ref[pl.ds(m * half + row, LEV, stride=ROWS), :]
            held_ref[row, m * LEV : (m + 1) * LEV, :] = value
            s1_ref[row, m * LEV : (m + 1) * LEV, :] = value * inc
    for row in range(ROWS // 2):
        pair = s1_ref[2 * row] + s1_ref[2 * row + 1]
        pair = pair + jnp.where((lane & 1) == 0, pltpu.roll(pair, LANES - 1, 1), pltpu.roll(pair, 1, 1))
        s2_ref[row] = pair * (0.25 * scales[1] / scales[0])
    for row in range(ROWS // 4):
        pair = s2_ref[2 * row] + s2_ref[2 * row + 1]
        pair = pair + jnp.where((lane & 2) == 0, pltpu.roll(pair, LANES - 2, 1), pltpu.roll(pair, 2, 1))
        s4_ref[row] = pair * (0.25 * scales[2] / scales[1])

    tiles = []
    for ref, factor in ((s1_ref, 1), (s2_ref, 2), (s4_ref, 4)):
        width = ITERS * factor
        first = last = jnp.zeros((PLANES, LANES), jnp.float32)
        for row in range(ROWS // factor):
            turned = pltpu.roll(ref[row], width * row, 1) if row else ref[row]
            first = jnp.where(in_range(lane, width * row, width), turned, first)
            last = jnp.where(in_range(lane, width * row - width, width), turned, last)
        tiles.append((first, last))
    even = (lane & 1) == 0
    blank = jnp.zeros((2, PLANES, LANES), jnp.float32)
    lon_ref[here] = blank
    lon_ref[lax.rem(here + 2, count)] = blank
    for side, to in ((0, lax.rem(here + count - 1, count)), (1, lax.rem(here + 1, count))):
        lon_ref[to, 0] = tiles[0][side]
        lon_ref[to, 1] = jnp.where(even, tiles[1][side], tiles[2][side])


def side_tiles(got_ref, lane):
    here, count = lax.axis_index("lon"), lax.axis_size("lon")
    even = (lane & 1) == 0
    out = []
    for of in (lax.rem(here + 1, count), lax.rem(here + count - 1, count)):
        mixed = got_ref[of, 1]
        out.append(
            (
                got_ref[of, 0],
                jnp.where(even, mixed, pltpu.roll(mixed, 1, 1)),
                jnp.where(even, pltpu.roll(mixed, LANES - 1, 1), mixed),
            )
        )
    return out


def beside(right, left, lane, width, row, shift=0):
    both = jnp.where(in_range(lane, width * row, LANES // 2), right, left)
    turn = (shift - width * row) % LANES
    return pltpu.roll(both, turn, 1) if turn else both


CORNER_PLACES = ((2, 1, 0), (2, 2, 20), (2, 3, 32), (1, 1, 42), (1, 2, 52), (1, 3, 58), (0, 1, 63), (0, 2, 68), (0, 3, 71))
SHIFTS = {(band, distance): shift for band, distance, shift in CORNER_PLACES}


def corner_kernel(got_ref, s1_ref, s2_ref, s4_ref, out0_ref, out1_ref):
    lane = lane_ids()
    even = (lane & 1) == 0
    is_odd = (lane * 0 + lax.rem(lax.axis_index("lat"), 2)) == 1
    right, left = side_tiles(got_ref, lane)

    def put(k, tail, head):
        out0_ref[k] = jnp.where(is_odd, head, tail)
        out1_ref[k] = jnp.where(is_odd, tail, head)

    for k in range(ITERS):
        put(k, s1_ref[ROWS - ITERS + k], s1_ref[k])
        tail = jnp.where(even, s2_ref[ROWS // 2 - ITERS + k], s4_ref[ROWS // 4 - ITERS + k])
        put(ITERS + k, tail, jnp.where(even, s2_ref[k], s4_ref[k]))
    made = []
    for tail in (True, False):
        tile = jnp.zeros((PLANES, LANES), jnp.float32)
        for band, distance, shift in CORNER_PLACES:
            factor = factors[band]
            width = factor * (ITERS - distance)
            row = ROWS // factor - distance if tail else distance - 1
            halo = beside(right[band], left[band], lane, ITERS * factor, row, shift)
            tile = jnp.where(in_range(lane, shift - width, 2 * width), halo, tile)
        made.append(tile)
    put(CORNER, *made)


def beside_sum(row, factor, lane, halves=(0, 1)):
    first, last = lane < factor, lane >= LANES - factor
    out = []
    for h in halves:
        up = pltpu.roll(jnp.where(last, row[1 - h], row[h]), factor, 1)
        down = pltpu.roll(jnp.where(first, row[1 - h], row[h]), LANES - factor, 1)
        out.append(up + down)
    return out


def combine(sums, coefficients):
    return sum(c * v for c, v in zip(coefficients, sums))


def inner_kernel(s1_ref, s2_ref, s4_ref, got_ref, *levels_and_sums):
    lane = lane_ids()
    right, left = side_tiles(got_ref, lane)
    bands = len(factors)
    levels, columns, halos = (levels_and_sums[bands * n : bands * (n + 1)] for n in range(3))
    for band, factor in enumerate(factors):
        level, own, column, halo, rows = levels[band], (s1_ref, s2_ref, s4_ref)[band], columns[band], halos[band], ROWS // factor
        for row in range(rows):
            halo[row] = beside(right[band], left[band], lane, ITERS * factor, row)
        for k in range(1, ITERS + 1):
            for row in range(rows):
                before = own[row] if k == 1 else column[k - 2, row]
                new = beside_sum((before, halo[row]), factor, lane, (0, 1) if k < ITERS else (0,))
                column[k - 1, row] = new[0]
                if k < ITERS:
                    halo[row] = new[1]
        for row in range(rows):
            sums = [own[row]] + [column[k, row] for k in range(ITERS)]
            for i in range(ITERS + 1):
                level[i, row] = combine(sums, POLY[band][i])
        for i in range(ITERS - 1, -1, -1):
            for row in range(ITERS - i, rows - ITERS + i):
                level[i, row] = level[i, row] + (level[i + 1, row - 1] + level[i + 1, row + 1])


def outer_kernel(held_ref, lat1_ref, lat0_ref, level1_ref, level2_ref, level4_ref, out_ref, edge_ref, ends_ref):
    lane = lane_ids()
    even = (lane & 1) == 0
    place, places = lax.axis_index("lat"), lax.axis_size("lat")
    odd = lax.rem(place, 2)
    edge_ref[0] = lat0_ref[...]
    edge_ref[1] = lat1_ref[...]
    for band, factor in enumerate(factors):
        level, rows = (level1_ref, level2_ref, level4_ref)[band], ROWS // factor
        for top in (True, False):
            edge = edge_ref.at[1 - odd] if top else edge_ref.at[odd]
            keep = jnp.where(place > 0 if top else place < places - 1, 1.0, 0.0).astype(jnp.float32)
            row_at = (lambda d: -d) if top else (lambda d: rows - 1 + d)
            outside = {}
            for distance in range(1, ITERS + 1):
                k = ITERS - distance if top else distance - 1
                if band == 0:
                    value = edge[k]
                else:
                    value = edge[ITERS + k]
                    turned = pltpu.roll(value, 1 if band == 1 else LANES - 1, 1)
                    value = jnp.where(even, value, turned) if band == 1 else jnp.where(even, turned, value)
                if distance < ITERS:
                    shift = SHIFTS[band, distance]
                    halo = pltpu.roll(edge[CORNER], LANES - shift, 1) if shift else edge[CORNER]
                    now, sums = (value, halo), [value]
                    for k in range(1, ITERS + 1 - distance):
                        now = beside_sum(now, factor, lane, (0, 1) if k < ITERS - distance else (0,))
                        sums.append(now[0])
                else:
                    sums = [value]
                outside[distance] = {i: combine(sums, POLY[band][i]) for i in range(distance, ITERS + 1)}
            latest = {row_at(d): outside[d][ITERS] for d in outside}
            for i in range(ITERS - 1, -1, -1):
                load = lambda row: latest[row] if row in latest else level[i + 1, row]
                new = {}
                for distance in range(i + 1 - ITERS, i + 1):
                    row = row_at(distance)
                    near = load(row - 1) + load(row + 1)
                    new[row] = (outside[distance][i] + near) * keep if distance > 0 else level[i, row] + near
                latest = new
            for row in range(ITERS):
                ends_ref[band, row if top else ITERS + row] = latest[row if top else rows - ITERS + row]

    def final(band, row):
        rows = ROWS // factors[band]
        if row < ITERS:
            return ends_ref[band, row]
        if row >= rows - ITERS:
            return ends_ref[band, row - rows + 2 * ITERS]
        return (level1_ref, level2_ref, level4_ref)[band][0, row]

    for row in range(ROWS):
        total = (final(0, row) + final(1, row // 2) + final(2, row // 4)) * held_ref[row]
        out_ref[pl.ds(row, LEV, stride=ROWS), :] = total[:LEV] + total[LEV:]


def tiles_of(*dims):
    return pltpu.VMEM(dims + (PLANES, LANES), jnp.float32)


def on_chip(kernel, name, out_shape, scratch_shapes=(), held_in=pltpu.VMEM, bundles=1000):
    several = isinstance(out_shape, tuple)
    spec = pl.BlockSpec(memory_space=pltpu.VMEM)

    def call(*operands):
        return pl.pallas_call(
            kernel,
            out_shape=out_shape,
            in_specs=[spec if held_in == pltpu.VMEM else pl.BlockSpec(memory_space=pl.ANY)] * len(operands),
            out_specs=(spec,) * len(out_shape) if several else spec,
            scratch_shapes=scratch_shapes,
            compiler_params=pltpu.CompilerParams(vmem_limit_bytes=GRANT),
            cost_estimate=pl.CostEstimate(flops=bundles * 4096, bytes_accessed=bundles * 1024, transcendentals=0),
            name=name,
        )(*[pltpu.with_memory_space_constraint(x, held_in) for x in operands])

    return call


def body(members, increment):
    columns = lax.axis_size("lon")
    parts = lax.axis_size("mem")
    rows_of = lax.axis_size("lat")
    held, s1, s2, s4, to_lon = on_chip(
        pack_kernel,
        "pack",
        (
            tiles_of(ROWS),
            tiles_of(ROWS),
            tiles_of(ROWS // 2),
            tiles_of(ROWS // 4),
            tiles_of(columns, 2),
        ),
        [
            pltpu.VMEM((2 * LEV * ROWS, LANES), jnp.bfloat16),
            pltpu.VMEM((LEV * ROWS, LANES), jnp.float32),
            pltpu.VMEM((2 * LEV * ROWS, LANES), jnp.float32),
            pltpu.SemaphoreType.DMA((3,)),
        ],
        held_in=pltpu.HBM,
    )(members.reshape(2 * LEV * ROWS, LANES), increment.reshape(LEV * ROWS, LANES))
    from_lon = lax.all_to_all(to_lon, "lon", 0, 0)
    out0, out1 = on_chip(corner_kernel, "corner", (tiles_of(EDGE), tiles_of(EDGE)))(from_lon, s1, s2, s4)
    swap0 = [(i, i ^ 1) for i in range(rows_of)]
    swap1 = [(i, ((i + 1) ^ 1) - 1) for i in range(1, rows_of - 1)]
    in1 = lax.ppermute(out1, "lat", swap1)
    in0 = lax.ppermute(out0, "lat", swap0)
    levels = on_chip(
        inner_kernel,
        "inner",
        tuple(tiles_of(ITERS + 1, ROWS // factor) for factor in factors),
        [tiles_of(ITERS, ROWS // factor) for factor in factors] + [tiles_of(ROWS // factor) for factor in factors],
        bundles=3000,
    )(s1, s2, s4, from_lon)
    partial_value = on_chip(
        outer_kernel,
        "outer",
        pltpu.VMEM((LEV * ROWS, LANES), jnp.float32),
        [tiles_of(2, EDGE), tiles_of(3, 2 * ITERS)],
    )(held, in1, in0, *levels)
    member_count = members.shape[0] * parts
    chunk = (parts, LEV * ROWS // parts, LANES)
    mine = jnp.sum(lax.all_to_all(partial_value.reshape(chunk), "mem", 0, 0), axis=0)
    mine = mine * (1.0 / (member_count - 1))
    whole = lax.all_to_all(jnp.broadcast_to(mine[None], chunk), "mem", 0, 0)
    return whole.reshape(LEV, ROWS, LANES)


def solution(mesh):
    return jax.shard_map(
        body,
        mesh=mesh,
        in_specs=(P("mem", None, "lat", "lon"), P(None, "lat", "lon")),
        out_specs=P(None, "lat", "lon"),
        check_vma=False,
    )
```
